512 devices in a mesh: ch: 128 (over y, z, core), grp: 4 (over x).
Axes of the slice: x: 4, y: 8, z: 8, core: 2. Of those that a mesh axis runs over, the one named last changes fastest.
Arguments:
- raw: bfloat16 [4, 1024, 2048], P('grp', 'ch'), may hold values from -400 to 400
- order: int32 [128, 16], P('ch'), may hold values from 0 to 15, each once within a row
- pair_blocks: int32 [128, 3], P('ch'), may hold values from -1 to 15, as said below
Outputs:
- corr: bfloat16 [2048, 3, 128, 256], P(('ch', 'grp'))
The draws below stay inside these ranges and needn't reach their ends.
Inputs may be any that keep to these rules, and one draw needn't show every extreme that they name: `pair_blocks`: row i names distinct blocks among i * 16 // 128 - 1, i * 16 // 128, i * 16 // 128 + 1 that lie in 0 .. 15; slot 0 is always i * 16 // 128; live slots come first and empty ones hold -1.
All inputs are finite; a program needn't handle non-finite values.
Results may differ from the reference program's by a relative error of at most 0.013.
Values may be sent and summed in bfloat16 or wider, within the bound.
A program may use at most 128 MiB of HBM per device.

```python
import math
import jax
import jax.numpy as jnp
from jax import lax

CH_DEV = 16
SRC = 128
SEG = 256
LAGS = 256
SMOOTH = 8
MAXP = 3
NSEG = 4
WINDOWS = 4
CHANNELS = 2048
NBLK = 16


def draw_raw(key, part):
    key_noise, key_chan, key_seg = jax.random.split(key, 3)
    full_shape = (WINDOWS, NSEG, SEG, CHANNELS)
    noise = jax.random.truncated_normal(key_noise, -6.0, 6.0, full_shape, jnp.float32)
    chan_scale = jnp.exp(jax.random.uniform(key_chan, (1, 1, 1, CHANNELS), jnp.float32, 0.0, math.log(10.0)))
    seg_scale = jnp.exp(jax.random.uniform(key_seg, (WINDOWS, NSEG, 1, 1), jnp.float32, 0.0, math.log(3.0)))
    values = noise * chan_scale * seg_scale
    return values.reshape(WINDOWS, NSEG * SEG, CHANNELS).astype(jnp.bfloat16)


def draw_pair_blocks(key, part):
    block_rows = CHANNELS // CH_DEV
    key_extra, key_swap = jax.random.split(key, 2)
    rows = jnp.arange(block_rows, dtype=jnp.int32)
    own_block = rows * CH_DEV // SRC
    extra = jax.random.randint(key_extra, (block_rows,), 0, 4, dtype=jnp.int32)
    swapped = jax.random.randint(key_swap, (block_rows,), 0, 2, dtype=jnp.int32)
    left_block = own_block - 1
    right_block = own_block + 1
    has_left = (extra % 2 == 1) & (left_block >= 0)
    has_right = (extra // 2 == 1) & (right_block < NBLK)
    left_first = has_left & (~has_right | (swapped == 0))
    second_slot = jnp.where(left_first, left_block, jnp.where(has_right, right_block, -1))
    third_slot = jnp.where(has_left & has_right, jnp.where(swapped == 0, right_block, left_block), -1)
    return jnp.stack([own_block, second_slot, third_slot], axis=1).astype(jnp.int32)


def setup_inputs(seed: int = 0) -> dict:
    seeds = jax.random.split(jax.random.key(seed), 4)
    raw = draw_raw(jax.random.fold_in(seeds[3], 71), 0)
    order = jax.vmap(lambda own: jax.random.permutation(own, CH_DEV))(jax.random.split(seeds[1], (CHANNELS // CH_DEV))).reshape((CHANNELS // CH_DEV, CH_DEV)).astype(jnp.int32)
    pair_blocks = draw_pair_blocks(jax.random.fold_in(seeds[3], 71), 0)
    return dict(raw=raw, order=order, pair_blocks=pair_blocks)


lag_scale = 1.0 / 16.0

def transform_tables(half_len, lag_count, smooth_half):
    samples = jnp.arange(half_len, dtype=jnp.int32)
    column = jnp.arange(2 * half_len, dtype=jnp.int32)
    freq = column % half_len + 1
    phase_fwd = samples[:, None] * freq[None, :] % (2 * half_len)
    angle_fwd = phase_fwd.astype(jnp.float32) * (math.pi / half_len)
    forward = jnp.where(column[None, :] < half_len, jnp.cos(angle_fwd), -jnp.sin(angle_fwd)).astype(jnp.bfloat16)
    lag_steps = jnp.arange(lag_count, dtype=jnp.int32) - lag_count // 2
    phase_inv = freq[:, None] * lag_steps[None, :] % (2 * half_len)
    angle_inv = phase_inv.astype(jnp.float32) * (math.pi / half_len)
    inverse = (jnp.where(column[:, None] < half_len, jnp.cos(angle_inv), -jnp.sin(angle_inv)) * lag_scale).astype(jnp.bfloat16)
    bins = jnp.arange(half_len, dtype=jnp.int32)
    smoothing = (jnp.abs(bins[:, None] - bins[None, :]) <= smooth_half).astype(jnp.float32) / (2 * smooth_half + 1)
    return (forward, inverse, smoothing)

def whiten(segments, forward, smoothing):
    half_len = segments.shape[-1]
    flat_rows = segments.reshape(-1, half_len)
    spectrum = jnp.dot(flat_rows, forward, preferred_element_type=jnp.float32)
    real_part = spectrum[:, :half_len]
    imag_part = spectrum[:, half_len:]
    power_bins = real_part * real_part + imag_part * imag_part
    smoothed = jnp.dot(power_bins, smoothing, precision=lax.Precision.HIGHEST)
    water_level = lax.optimization_barrier(jnp.mean(power_bins, axis=1, keepdims=True))
    divisor = jnp.sqrt(smoothed + 0.1 * water_level + 1e-06)
    whitened = spectrum / jnp.concatenate([divisor, divisor], axis=1)
    return whitened.astype(jnp.bfloat16).reshape(segments.shape[:-1] + (2 * half_len,))

def correlate(receivers, sources, inverse):
    half_len = receivers.shape[-1] // 2
    seg_count = receivers.shape[1]
    recv_re = receivers[..., :half_len].astype(jnp.float32)
    recv_im = receivers[..., half_len:].astype(jnp.float32)
    left_first = jnp.concatenate([recv_re, recv_im], axis=1)
    left_second = jnp.concatenate([recv_im, -recv_re], axis=1)
    right_both = jnp.concatenate([sources[..., :half_len], sources[..., half_len:]], axis=1).astype(jnp.float32)
    cross_re = jnp.einsum('rnk,snk->rsk', left_first, right_both)
    cross_im = jnp.einsum('rnk,snk->rsk', left_second, right_both)
    cross_spec = (jnp.concatenate([cross_re, cross_im], axis=2) * (1.0 / seg_count)).astype(jnp.bfloat16)
    recv_count = receivers.shape[0]
    src_count = sources.shape[0]
    lag_values = jnp.dot(cross_spec.reshape(-1, 2 * half_len), inverse, preferred_element_type=jnp.float32)
    return lag_values.reshape(recv_count, src_count, inverse.shape[1])

def reference(raw, order, pair_blocks):
    forward, inverse, smoothing = transform_tables(SEG, LAGS, SMOOTH)
    block_count = CHANNELS // CH_DEV
    destination = (jnp.arange(block_count, dtype=jnp.int32)[:, None] * CH_DEV + order).reshape(-1).astype(jnp.int32)
    series = jnp.zeros(raw.shape, raw.dtype).at[:, :, destination].set(raw)
    series = jnp.transpose(series, (0, 2, 1)).reshape(WINDOWS, CHANNELS, NSEG, SEG)
    whitened = whiten(series, forward, smoothing)

    def one_device(device_index):
        receivers = lax.dynamic_slice_in_dim(whitened, (device_index * CH_DEV).astype(jnp.int32), CH_DEV, 1)
        slot_results = []
        for slot_index in range(MAXP):
            block_id = pair_blocks[device_index, slot_index]
            is_live = (block_id >= 0).astype(jnp.float32)
            source_start = (jnp.maximum(block_id, 0) * SRC).astype(jnp.int32)
            sources = lax.dynamic_slice_in_dim(whitened, source_start, SRC, 1)
            total = jnp.zeros((CH_DEV, SRC, LAGS), jnp.float32)
            for window_index in range(WINDOWS):
                lag_values = correlate(receivers[window_index], sources[window_index], inverse)
                total = total + (lag_values * is_live).astype(jnp.bfloat16).astype(jnp.float32)
            slot_results.append(total)
        stacked = jnp.stack(slot_results, axis=1)
        return (stacked / WINDOWS).astype(jnp.bfloat16)
    result = lax.map(one_device, jnp.arange(block_count, dtype=jnp.int32))
    return result.reshape(CHANNELS, MAXP, SRC, LAGS)
```

```python
import math

import jax
import jax.numpy as jnp
import numpy as np
from jax import lax
from jax.experimental import pallas as pl
from jax.experimental.pallas import tpu as pltpu
from jax.sharding import PartitionSpec as P

CH_DEV = 16
SRC = 128
SEG = 256
LAGS = 256
SMOOTH = 8
MAXP = 3
NSEG = 4
WINDOWS = 4
ROWS = 8
Y, Z, C = 8, 8, 2
RECV = 4
WIDE = 512
SPAN = 384
BINS = 16
NWS = WINDOWS * NSEG
BF16 = jnp.bfloat16
F32 = jnp.float32
MESH = pl.DeviceIdType.MESH


def tables():
    place = np.arange(SEG)
    zc, parity, row = place // 16, place // 8 % 2, place % 8
    sample = parity * 128 + zc * 8 + row
    column = np.arange(2 * SEG)
    freq = column % SEG + 1
    angle = (sample[None, :] * freq[:, None] % (2 * SEG)) * (math.pi / SEG)
    real = column[:, None] < SEG
    forward = np.where(real, np.cos(angle), -np.sin(angle))
    lag = np.arange(LAGS) - LAGS // 2
    angle = (freq[None, :] * lag[:, None] % (2 * SEG)) * (math.pi / SEG)
    inverse = np.where(real.T, np.cos(angle), -np.sin(angle)) / 16.0
    return jnp.asarray(forward, BF16), jnp.asarray(inverse, BF16)


def start_block(y):
    return jnp.clip(2 * y - 1, 0, 12)


def first_lane_block(y, half):
    return jnp.where(y == 0, 0, jnp.where(y == Y - 1, 1, half))


def gather_kernel(raw, order, buf, ords, tile, y_send, y_recv, o_send, o_recv, q_send, q_recv, z_send, z_recv, p_send, p_recv, x_send, x_recv, own_sem):
    i = lax.axis_index("ch")
    x = lax.axis_index("grp")
    y, z, c = i // 16, i // 2 % Z, i % 2
    half = z // 4

    def ch(yy, zz, cc):
        return (yy * Z + zz) * C + cc

    def peer(yy, zz, cc, xx):
        return {"ch": ch(yy, zz, cc), "grp": xx}

    barrier = pltpu.get_barrier_semaphore()
    peers = [peer((y + d) % Y, z, c, x) for d in range(1, Y)]
    row = []
    for d in range(Z):
        for e in range(C):
            if d or e:
                row.append((d, e))
    peers += [peer(y, (z + d) % Z, (c + e) % C, x) for d, e in row]
    peers += [peer(y, z, c, (x + 1) % WINDOWS), peer(y, z, c, (x + 3) % WINDOWS)]
    for device in peers:
        pl.semaphore_signal(barrier, inc=1, device_id=device, device_id_type=MESH)

    base = i % 8 * CH_DEV
    lanes = lax.broadcasted_iota(jnp.int32, (16, 128), 1)
    placed = jnp.zeros((16, 128), jnp.int32)
    for j in range(CH_DEV):
        placed = jnp.where(lanes == base + j, base + order[0, j], placed)
    tile[0] = placed.astype(F32).astype(BF16)

    pl.semaphore_wait(barrier, len(peers))

    sends = []

    def send(src, dst, s_sem, r_sem, device):
        copy = pltpu.make_async_remote_copy(
            src_ref=src, dst_ref=dst, send_sem=s_sem, recv_sem=r_sem, device_id=device, device_id_type=MESH
        )
        copy.start()
        sends.append(copy)
        return copy

    seg, parity = y // 2, y % 2

    def landing():
        return buf.at[x, z, c, seg, pl.ds(pl.multiple_of(parity * ROWS, ROWS), ROWS), :]

    def wanted(yy):
        return raw.at[0, :, pl.ds(pl.multiple_of(start_block(yy) * SRC, SRC), WIDE)]

    waits = []
    for d in range(1, Y):
        yy = (y + d) % Y
        waits.append(send(wanted(yy), landing(), y_send.at[d - 1], y_recv.at[d - 1], peer(yy, z, c, x)))
    toward = (y + jnp.where(half == 1, 1, Y - 1)) % Y
    order_copy = send(tile.at[0], tile.at[1], o_send.at[0], o_recv.at[0], peer(toward, z, c, x))
    own = pltpu.make_async_copy(wanted(y), landing(), own_sem)
    own.start()

    order_copy.wait_recv()
    order_waits = []
    for n, (d, e) in enumerate(row):
        order_waits.append(
            send(tile, ords.at[z, c], q_send.at[n], q_recv.at[n], peer(y, (z + d) % Z, (c + e) % C, x))
        )
    own_order = pltpu.make_async_copy(tile, ords.at[z, c], o_send.at[1])
    own_order.start()

    for copy in waits:
        copy.wait_recv()
    own.wait()

    lane = pl.ds(pl.multiple_of(first_lane_block(y, half) * SRC, SRC), SPAN)

    def part(w, zz, cc, first=0, count=NSEG):
        return buf.at[w, zz, cc, pl.ds(first, count), :, lane]

    received = {}

    def to_partner(w_rel, d):
        w, zz = (x + w_rel) % WINDOWS, (z + d) % Z
        n = w_rel * Z + d
        copy = send(part(w, zz, c), part(w, zz, c), p_send.at[n], p_recv.at[n], peer(y, z, (c + 1) % C, x))
        received["p", n] = copy

    def to_x(d):
        zz = (z + d) % Z
        for side, step in ((0, 1), (1, WINDOWS - 1)):
            copy = send(
                part(x, zz, c), part(x, zz, c), x_send.at[side, d], x_recv.at[side, d], peer(y, z, c, (x + step) % WINDOWS)
            )
            received["x", side, d] = copy

    def forward_x(d):
        zz = (z + d) % Z
        for side, w_rel, step, first in ((0, WINDOWS - 1, 1, 0), (1, 1, WINDOWS - 1, 2)):
            received["x", side, d].wait_recv()
            w = (x + w_rel) % WINDOWS
            copy = send(
                part(w, zz, c, first, 2),
                part(w, zz, c, first, 2),
                x_send.at[2 + side, d],
                x_recv.at[2 + side, d],
                peer(y, z, c, (x + step) % WINDOWS),
            )
            received["x", 2 + side, d] = copy
            to_partner(w_rel, d)

    def along_z(side, hop, zz, first, count):
        step = 1 if side == 0 else Z - 1
        ref = buf.at[x, zz, c, pl.ds(first, count)]
        copy = send(ref, ref, z_send.at[side, hop - 1], z_recv.at[side, hop - 1], peer(y, (z + step) % Z, c, x))
        received["z", side, hop] = copy

    along_z(0, 1, z, 0, NSEG)
    along_z(1, 1, z, 0, NSEG)
    to_x(0)
    to_partner(0, 0)
    for hop in range(1, 4):
        for side, d in ((0, Z - hop), (1, hop)):
            received["z", side, hop].wait_recv()
            zz = (z + d) % Z
            if hop < 3:
                along_z(side, hop + 1, zz, 0, NSEG)
            else:
                along_z(side, hop + 1, zz, 2 * side, 2)
            to_x(d)
            to_partner(0, d)
    received["z", 0, 4].wait_recv()
    received["z", 1, 4].wait_recv()
    to_x(4)
    to_partner(0, 4)

    arrival = [0, 7, 1, 6, 2, 5, 3, 4]
    for d in arrival:
        forward_x(d)
    for d in arrival:
        received["x", 2, d].wait_recv()
        received["x", 3, d].wait_recv()
        to_partner(2, d)
    for w_rel in (0, 1, 3, 2):
        for d in range(Z):
            received["p", w_rel * Z + d].wait_recv()
    for copy in order_waits:
        copy.wait_recv()
    own_order.wait()
    for copy in sends:
        copy.wait_send()


def gather(raw, order):
    dma = pltpu.SemaphoreType.DMA
    return pl.pallas_call(
        gather_kernel,
        out_shape=(
            jax.ShapeDtypeStruct((WINDOWS, Z, C, NSEG, 16, WIDE), BF16),
            jax.ShapeDtypeStruct((Z, C, 2, 16, 128), BF16),
        ),
        in_specs=[pl.BlockSpec(memory_space=pltpu.VMEM), pl.BlockSpec(memory_space=pltpu.SMEM)],
        out_specs=[pl.BlockSpec(memory_space=pltpu.VMEM)] * 2,
        scratch_shapes=[
            pltpu.VMEM((2, 16, 128), BF16),
            dma((Y - 1,)),
            dma((Y - 1,)),
            dma((2,)),
            dma((1,)),
            dma((15,)),
            dma((15,)),
            dma((2, 4)),
            dma((2, 4)),
            dma((WINDOWS * Z,)),
            dma((WINDOWS * Z,)),
            dma((4, Z)),
            dma((4, Z)),
            dma,
        ],
        compiler_params=pltpu.CompilerParams(collective_id=0, has_side_effects=True, vmem_limit_bytes=32 << 20),
        name="gather",
    )(raw, order)


def dot(a, b, dims=((1,), (0,))):
    return lax.dot_general(a, b, (dims, ((), ())), preferred_element_type=F32)


NT = ((1,), (1,))


def correlate_kernel(pairs, place, buf, ords, forward, inverse, out, white, pos, left, cross, lagged):
    y, half, block, g, first = place[0], place[1], place[2], place[3], place[4]
    start = start_block(y) + first
    lane = pl.multiple_of(first * SRC, SRC)

    for n, (upper, which) in enumerate(((1, 1), (0, 0), (1, 0), (0, 1))):
        total = jnp.zeros((16, 128), F32)
        for zz in range(4):
            for cc in range(C):
                total = total + ords[upper * 4 + zz, cc, which].astype(F32)
        pos[n] = total

    def iota(shape, axis):
        return lax.broadcasted_iota(jnp.int32, shape, axis)

    band = (jnp.abs(iota((SEG, SEG), 0) - iota((SEG, SEG), 1)) <= SMOOTH).astype(F32).astype(BF16)

    def whiten(ws, carry):
        w, seg = ws // NSEG, ws % NSEG
        samples = buf[w, :, :, seg, :, pl.ds(lane, SPAN)].reshape(SEG, SPAN)
        spectrum = dot(forward[...], samples)
        real, imag = spectrum[:SEG], spectrum[SEG:]
        power = real * real + imag * imag
        level = jnp.sum(power, axis=0, keepdims=True) * (0.1 / SEG)
        smoothed = dot(band, power.astype(BF16)) * (1.0 / (2 * SMOOTH + 1))
        scale = lax.rsqrt(smoothed + level + 1e-6)
        white[ws, :SEG] = (real * scale).astype(BF16)
        white[ws, SEG:] = (imag * scale).astype(BF16)
        return carry

    lax.fori_loop(0, NWS, whiten, 0)

    mine = pos[1 + half][:1].astype(jnp.int32)
    rows = iota((128, 128), 0)
    target = block % 8 * CH_DEV + g * RECV + rows // 16
    hit = (mine == target) & (rows < RECV * NWS)
    own_lane = pl.multiple_of((block // 8 - start) * SRC, SRC)

    def pick(ws, total):
        choice = (hit & (rows % 16 == ws)).astype(F32).astype(BF16)
        return total + dot(white[ws, :, pl.ds(own_lane, SRC)], choice, NT)

    picked = lax.fori_loop(0, NWS, pick, jnp.zeros((2 * SEG, 128), F32)).astype(BF16)
    expand = (iota((128, RECV * 256), 0) == iota((128, RECV * 256), 1) // 16).astype(F32).astype(BF16)
    keep = iota((2 * SEG, RECV * 256), 0) % BINS == iota((2 * SEG, RECV * 256), 1) % BINS
    left[...] = jnp.where(keep, dot(picked, expand), 0.0).astype(BF16)

    def bins(q, carry):
        at = pl.multiple_of(q * BINS, BINS)
        re = left[pl.ds(at, BINS), :]
        im = left[pl.ds(SEG + at, BINS), :]
        lhs = []
        for r in range(RECV):
            one = slice(r * 256, r * 256 + 256)
            lhs.append(jnp.concatenate([re[:, one], im[:, one]], axis=1))
            lhs.append(jnp.concatenate([im[:, one], -re[:, one]], axis=1))
        lhs = jnp.concatenate(lhs, axis=0)
        right_re = white[:, pl.ds(at, BINS), :].reshape(256, SPAN)
        right_im = white[:, pl.ds(SEG + at, BINS), :].reshape(256, SPAN)
        right = jnp.concatenate([right_re, right_im], axis=0)
        product = (dot(lhs, right) * (1.0 / (NSEG * WINDOWS))).astype(BF16)
        for r in range(RECV):
            cross[r, pl.ds(at, BINS), :] = product[r * 2 * BINS : r * 2 * BINS + BINS]
            cross[r, pl.ds(SEG + at, BINS), :] = product[r * 2 * BINS + BINS : (r + 1) * 2 * BINS]
        return carry

    lax.fori_loop(0, SEG // BINS, bins, 0)

    for r in range(RECV):
        value = dot(inverse[...], cross[r]).astype(BF16)
        for n in range(SPAN // SRC):
            lagged[n, r] = value[:, n * SRC : n * SRC + SRC]

    for p in range(MAXP):
        b = pairs[0, p]
        live = b >= 0
        source = jnp.where(live, b - start, 0)
        where_to = pos[jnp.where(live, b - (2 * y - 1), 1)][:1].astype(jnp.int32)
        turn = ((iota((SRC, SRC), 0) == where_to) & live).astype(F32).astype(BF16)
        for r in range(RECV):
            out[r, p] = dot(turn, lagged[source, r], NT).astype(BF16)


def correlate(pairs, place, buf, ords, forward, inverse):
    smem = pl.BlockSpec(memory_space=pltpu.SMEM)
    vmem = pl.BlockSpec(memory_space=pltpu.VMEM)
    return pl.pallas_call(
        correlate_kernel,
        out_shape=jax.ShapeDtypeStruct((RECV, MAXP, SRC, LAGS), BF16),
        in_specs=[smem, smem, vmem, vmem, vmem, vmem],
        out_specs=vmem,
        scratch_shapes=[
            pltpu.VMEM((NWS, 2 * SEG, SPAN), BF16),
            pltpu.VMEM((4, 16, 128), F32),
            pltpu.VMEM((2 * SEG, RECV * 256), BF16),
            pltpu.VMEM((RECV, 2 * SEG, SPAN), BF16),
            pltpu.VMEM((SPAN // SRC, RECV, LAGS, SRC), BF16),
        ],
        compiler_params=pltpu.CompilerParams(vmem_limit_bytes=48 << 20),
        name="correlate",
    )(pairs, place, buf, ords, forward, inverse)


def local(raw, order, pair_blocks):
    buf, ords = gather(raw, order)
    forward, inverse = tables()
    i, g = lax.axis_index("ch"), lax.axis_index("grp")
    y, half = i // 16, i // 8 % 2
    place = jnp.stack([y, half, i, g, first_lane_block(y, half)]).astype(jnp.int32)
    return correlate(pair_blocks, place, buf, ords, forward, inverse)


def solution(mesh):
    placed = (P("grp", "ch", None), P("ch", None), P("ch", None))
    return jax.shard_map(
        local,
        mesh=mesh,
        in_specs=placed,
        out_specs=P(("ch", "grp"), None, None, None),
        check_vma=False,
    )
```
